32 devices in a mesh: vocab: 8 (over y, x, core), hidden: 4 (over z).
Axes of the slice: x: 2, y: 2, z: 4, core: 2. Of those that a mesh axis runs over, the one named last changes fastest.
Arguments:
- token_ids: int32 [4096], P('vocab'), may hold values from 0 to 30719
- table: bfloat16 [30720, 128], P('vocab'), may hold values from -0.25 to 0.25
- projection: bfloat16 [128, 4096], P(None, 'hidden'), may hold values from -0.09375 to 0.09375
- grad_out: bfloat16 [4096, 4096], P('vocab', 'hidden'), may hold values from -6 to 6
Outputs:
- table_grad: float32 [30720, 128], P('vocab', 'hidden')
- projection_grad: float32 [128, 4096], P(None, 'hidden')
The draws below stay inside these ranges and needn't reach their ends.
All inputs are finite; a program needn't handle non-finite values.
Results may differ from the reference program's by a relative error of at most 0.018.
Values may be sent and summed in bfloat16 or wider, within the bound.
A program may use at most 64 MiB of HBM per device.

```python
import jax
import jax.numpy as jnp

D_E = 128
HID = 4096
VOCAB = 30720
TOKENS = 4096
N_HIDDEN = 4


def with_ends(values, key, low, largest):
    spot = [jax.random.randint(jax.random.fold_in(key, axis), (), 0, length) for axis, length in enumerate(values.shape)]
    widest = values.shape.index(max(values.shape))
    next_to = spot[:widest] + [(spot[widest] + 1) % values.shape[widest]] + spot[widest + 1:]
    return values.at[tuple(spot)].set(low).at[tuple(next_to)].set(largest)


def block_levels(own_key, extent, shards, low, largest):
    gain = 1.0
    for axis_at, shards_of in shards:
        heights = jax.random.uniform(jax.random.fold_in(jax.random.fold_in(own_key, 6), axis_at), (shards_of,), jnp.float32, low / len(shards), largest / len(shards))
        gain = gain * jnp.repeat(jnp.exp(heights), extent[axis_at] // shards_of).reshape((-1,) + (1,) * (len(extent) - 1 - axis_at))
    return gain


def noise(key, extent, scale, most, pieces=(), kind=jnp.bfloat16):
    drawn = scale * jax.random.normal(key, extent, jnp.float32)
    if pieces:
        drawn = drawn * block_levels(key, extent, pieces, -0.22, 0.18)
    return jnp.clip(drawn, -most, most).astype(kind)


def setup_inputs(seed: int = 0) -> dict:
    arg_keys = jax.random.split(jax.random.key(seed), 5)
    token_ids = with_ends(jax.random.randint(arg_keys[0], (TOKENS,), 0, VOCAB), jax.random.fold_in(arg_keys[0], 1), 0, VOCAB - 1).astype(jnp.int32)
    table = noise(arg_keys[1], (VOCAB, D_E), (TOKENS ** -0.5), 0.25, ((0, 8),))
    projection = noise(arg_keys[2], (D_E, HID), HID ** -0.5, 0.09375, ((1, 4),))
    grad_out = noise(arg_keys[3], (TOKENS, HID), 1.0, 6.0, ((0, 8), (1, 4)))
    return dict(token_ids=token_ids, table=table, projection=projection, grad_out=grad_out)


def reference(token_ids, table, projection, grad_out):
    embedded = jnp.take(table, token_ids, axis=0)
    projection_grad = jnp.dot(embedded.T, grad_out, preferred_element_type=jnp.float32)
    width = HID // N_HIDDEN
    total = jnp.zeros((grad_out.shape[0], projection.shape[0]), jnp.float32)
    for index in range(N_HIDDEN):
        part_out = grad_out[:, index * width:(index + 1) * width]
        part_proj = projection[:, index * width:(index + 1) * width]
        partial_value = jnp.dot(part_out, part_proj.T, preferred_element_type=jnp.float32)
        total = total + partial_value.astype(jnp.bfloat16).astype(jnp.float32)
    token_grad = total.astype(jnp.bfloat16)
    table_grad = jax.ops.segment_sum(token_grad.astype(jnp.float32), token_ids, num_segments=VOCAB)
    return table_grad, projection_grad
```

```python
import functools

import jax
import jax.numpy as jnp
from jax import lax
from jax.experimental import pallas as pl
from jax.experimental.pallas import tpu as pltpu
from jax.sharding import PartitionSpec as P

MESH = pl.DeviceIdType.MESH
SPAN = 256
NT = (((1,), (1,)), ((), ()))


def kernel(
    nv, nh, ids_ref, table_hbm, proj_hbm, grad_hbm, rows_out, proj_out,
    table, proj, grad, ids_all, part, part_in, tg_own, tg_all, quarter_t, one_hot, spread,
    found, found_in, emb, pg, pg_in, pg_own, pg_all,
    load_sem, ids_s, ids_r, part_s, part_r, tg_s, tg_r, found_s, found_r, emb_s, emb_r, pg_s, pg_r, all_s, all_r,
):
    v = lax.axis_index("vocab")
    h = lax.axis_index("hidden")
    rows, width = table.shape
    tokens = grad.shape[0]
    cols = width // nh
    groups = pl.cdiv(rows, SPAN)
    chunk = width // nv

    loads = [
        pltpu.make_async_copy(src, dst, load_sem.at[i])
        for i, (src, dst) in enumerate(((proj_hbm, proj), (grad_hbm, grad), (table_hbm, table)))
    ]
    for load in loads:
        load.start()

    def at_v(k):
        return lax.rem(v + k, nv)

    def at_h(k):
        return lax.rem(h + k, nh)

    barrier = pltpu.get_barrier_semaphore()
    for k in range(1, nv):
        pl.semaphore_signal(barrier, inc=1, device_id={"vocab": at_v(k)}, device_id_type=MESH)
    for k in range(1, nh):
        pl.semaphore_signal(barrier, inc=1, device_id={"hidden": at_h(k)}, device_id_type=MESH)
    pl.semaphore_wait(barrier, nv + nh - 2)

    def send(src, dst, s, r, k, where):
        copy = pltpu.make_async_remote_copy(
            src_ref=src, dst_ref=dst, send_sem=s.at[k - 1], recv_sem=r.at[k - 1],
            device_id=where, device_id_type=MESH,
        )
        copy.start()
        return copy

    sent = []
    ids_c = [send(ids_ref, ids_all.at[v], ids_s, ids_r, k, {"vocab": at_v(k)}) for k in range(1, nv)]
    ids_all[v] = ids_ref[...]

    loads[0].wait()
    loads[1].wait()
    partial_t = lax.dot_general(proj[...], grad[...], NT, preferred_element_type=jnp.float32)
    for j in range(nh):
        part[j] = partial_t[j * cols:(j + 1) * cols].astype(jnp.bfloat16)
    part_c = [
        send(part.at[at_h(k)], part_in.at[h], part_s, part_r, k, {"hidden": at_h(k)}) for k in range(1, nh)
    ]

    loads[2].wait()
    pick = (
        lax.broadcasted_iota(jnp.int32, (cols, width), 1)
        == lax.broadcasted_iota(jnp.int32, (cols, width), 0) + h * cols
    ).astype(jnp.float32).astype(jnp.bfloat16)
    turned = []
    for g in range(groups):
        size = min(SPAN, rows - g * SPAN)
        piece = lax.dot_general(
            pick, table[g * SPAN:g * SPAN + size], NT, preferred_element_type=jnp.float32
        )
        if size < SPAN:
            piece = jnp.concatenate([piece, jnp.zeros((cols, SPAN - size), jnp.float32)], axis=1)
        turned.append(piece)
    quarter_t[...] = jnp.concatenate(turned, axis=0).astype(jnp.bfloat16)

    def look_up(j):
        rel = ids_all[j] - v * rows
        group = lax.shift_right_arithmetic(rel, SPAN.bit_length() - 1)
        low = jnp.bitwise_and(rel, SPAN - 1)
        hot = (lax.broadcasted_iota(jnp.int32, (SPAN, tokens), 0) == low).astype(jnp.float32).astype(jnp.bfloat16)
        one_hot[:, pl.ds(pl.multiple_of(j * tokens, tokens), tokens)] = hot
        picked = jnp.dot(quarter_t[...], hot, preferred_element_type=jnp.float32)
        total = jnp.zeros((cols, tokens), jnp.float32)
        for g in range(groups):
            total = total + jnp.where(group == g, picked[g * cols:(g + 1) * cols], 0.0)
        found[j] = total.astype(jnp.bfloat16)

    found_c = []
    for k in range(1, nv):
        ids_c[k - 1].wait_recv()
        j = at_v(nv - k)
        look_up(j)
        found_c.append(send(found.at[j], found_in.at[v], found_s, found_r, k, {"vocab": j}))
    look_up(v)

    for copy in part_c:
        copy.wait_recv()
    part_in[h] = part[h]
    token_grad = part_in[0].astype(jnp.float32)
    for j in range(1, nh):
        token_grad = token_grad + part_in[j].astype(jnp.float32)
    tg_own[...] = token_grad.astype(jnp.bfloat16)
    tg_c = [send(tg_own, tg_all.at[v], tg_s, tg_r, k, {"vocab": at_v(k)}) for k in range(1, nv)]
    tg_all[v] = tg_own[...]

    for copy in found_c:
        copy.wait_recv()
    found_in[v] = found[v]
    mine = found_in[0].astype(jnp.float32)
    for j in range(1, nv):
        mine = mine + found_in[j].astype(jnp.float32)
    emb[h] = mine.astype(jnp.bfloat16)
    emb_c = [send(emb.at[h], emb.at[h], emb_s, emb_r, k, {"hidden": at_h(k)}) for k in range(1, nh)]
    for copy in emb_c:
        copy.wait_recv()
    embedded = jnp.concatenate([emb[j].astype(jnp.float32) for j in range(nh)], axis=0).astype(jnp.bfloat16)
    partial_proj = jnp.dot(embedded, grad[...], preferred_element_type=jnp.float32)
    for j in range(nv):
        pg[j] = partial_proj[j * chunk:(j + 1) * chunk].astype(jnp.bfloat16)
    pg_c = [send(pg.at[at_v(k)], pg_in.at[v], pg_s, pg_r, k, {"vocab": at_v(k)}) for k in range(1, nv)]

    for copy in tg_c:
        copy.wait_recv()
    for j in range(nv):
        rel = ids_all[j] - v * rows
        group = lax.shift_right_arithmetic(rel, SPAN.bit_length() - 1)
        value = tg_all[j].astype(jnp.float32)
        spread[:, j * tokens:(j + 1) * tokens] = jnp.concatenate(
            [jnp.where(group == g, value, 0.0) for g in range(groups)], axis=0
        ).astype(jnp.bfloat16)
    summed = lax.dot_general(spread[...], one_hot[...], NT, preferred_element_type=jnp.float32)
    for g in range(groups):
        size = min(SPAN, rows - g * SPAN)
        rows_out[:, g * SPAN:g * SPAN + size] = summed[g * cols:(g + 1) * cols, :size]

    for copy in pg_c:
        copy.wait_recv()
    pg_in[v] = pg[v]
    total = pg_in[0].astype(jnp.float32)
    for j in range(1, nv):
        total = total + pg_in[j].astype(jnp.float32)
    pg_own[...] = total.astype(jnp.bfloat16)
    all_c = [send(pg_own, pg_all.at[v], all_s, all_r, k, {"vocab": at_v(k)}) for k in range(1, nv)]
    pg_all[v] = pg_own[...]
    for copy in all_c:
        copy.wait_recv()
    proj_out[...] = pg_all[...]
    for copy in ids_c + part_c + tg_c + found_c + emb_c + pg_c + all_c:
        copy.wait_send()


def solution(mesh):
    nv, nh = mesh.shape["vocab"], mesh.shape["hidden"]

    def on_device(token_ids, table, projection, grad_out):
        rows, width = table.shape
        tokens, hid = grad_out.shape
        cols, chunk = width // nh, width // nv
        stacked = pl.cdiv(rows, SPAN) * cols
        half = jnp.bfloat16
        vmem = pl.BlockSpec(memory_space=pltpu.VMEM)
        hbm = pl.BlockSpec(memory_space=pl.ANY)
        sems = [pltpu.SemaphoreType.DMA((3,))]
        for peers in (nv, nh, nv, nv, nh, nv, nv):
            sems += [pltpu.SemaphoreType.DMA((peers - 1,))] * 2
        rows_t, proj_grad = pl.pallas_call(
            functools.partial(kernel, nv, nh),
            out_shape=(
                jax.ShapeDtypeStruct((cols, rows), jnp.float32),
                jax.ShapeDtypeStruct((nv, chunk, hid), half),
            ),
            in_specs=[vmem, hbm, hbm, hbm],
            out_specs=(vmem, vmem),
            scratch_shapes=[
                pltpu.VMEM((rows, width), half),
                pltpu.VMEM((width, hid), half),
                pltpu.VMEM((tokens, hid), half),
                pltpu.VMEM((nv, 1, tokens), jnp.int32),
                pltpu.VMEM((nh, cols, tokens), half),
                pltpu.VMEM((nh, cols, tokens), half),
                pltpu.VMEM((cols, tokens), half),
                pltpu.VMEM((nv, cols, tokens), half),
                pltpu.VMEM((stacked, SPAN), half),
                pltpu.VMEM((SPAN, nv * tokens), half),
                pltpu.VMEM((stacked, nv * tokens), half),
                pltpu.VMEM((nv, cols, tokens), half),
                pltpu.VMEM((nv, cols, tokens), half),
                pltpu.VMEM((nh, cols, tokens), half),
                pltpu.VMEM((nv, chunk, hid), half),
                pltpu.VMEM((nv, chunk, hid), half),
                pltpu.VMEM((chunk, hid), half),
                pltpu.VMEM((nv, chunk, hid), half),
            ] + sems,
            compiler_params=pltpu.CompilerParams(collective_id=0, has_side_effects=True),
        )(token_ids.reshape(1, tokens), table, projection, grad_out)
        return rows_t.T, proj_grad.reshape(width, hid).astype(jnp.float32)

    placed = (P("vocab"), P("vocab", None), P(None, "hidden"), P("vocab", "hidden"))
    return jax.shard_map(
        on_device,
        mesh=mesh,
        in_specs=placed,
        out_specs=(P("vocab", "hidden"), P(None, "hidden")),
        check_vma=False,
    )
```

```python
import functools

import jax
import jax.numpy as jnp
from jax import lax
from jax.experimental import pallas as pl
from jax.experimental.pallas import tpu as pltpu
from jax.sharding import PartitionSpec as P

MESH = pl.DeviceIdType.MESH
SPAN = 256
NT = (((1,), (1,)), ((), ()))


def kernel(
    nv, nh, ids_ref, table_hbm, proj_hbm, grad_hbm, rows_out, proj_out,
    table, proj, grad, ids_all, part, part_in, tg_own, tg_all, quarter_t, one_hot, spread,
    found, found_in, emb, pg, pg_in, pg_own, pg_all,
    load_sem, ids_s, ids_r, part_s, part_r, tg_s, tg_r, found_s, found_r, emb_s, emb_r, pg_s, pg_r, all_s, all_r,
):
    v = lax.axis_index("vocab")
    h = lax.axis_index("hidden")
    rows, width = table.shape
    tokens = grad.shape[0]
    cols = width // nh
    groups = pl.cdiv(rows, SPAN)
    chunk = grad.shape[1] // nv
    nearest = sorted(range(1, nh), key=lambda k: min(k, nh - k))

    loads = [
        pltpu.make_async_copy(src, dst, load_sem.at[i])
        for i, (src, dst) in enumerate(((proj_hbm, proj), (grad_hbm, grad), (table_hbm, table)))
    ]
    for load in loads:
        load.start()

    def at_v(k):
        return lax.rem(v + k, nv)

    def at_h(k):
        return lax.rem(h + k, nh)

    barrier = pltpu.get_barrier_semaphore()
    for k in range(1, nv):
        pl.semaphore_signal(barrier, inc=1, device_id={"vocab": at_v(k)}, device_id_type=MESH)
    for k in range(1, nh):
        pl.semaphore_signal(barrier, inc=1, device_id={"hidden": at_h(k)}, device_id_type=MESH)
    pl.semaphore_wait(barrier, nv + nh - 2)

    def send(src, dst, s, r, k, where):
        copy = pltpu.make_async_remote_copy(
            src_ref=src, dst_ref=dst, send_sem=s.at[k - 1], recv_sem=r.at[k - 1],
            device_id=where, device_id_type=MESH,
        )
        copy.start()
        return copy

    sent = []
    ids_c = [send(ids_ref, ids_all.at[v], ids_s, ids_r, k, {"vocab": at_v(k)}) for k in range(1, nv)]
    ids_all[v] = ids_ref[...]

    loads[0].wait()
    loads[1].wait()
    partial_t = lax.dot_general(proj[...], grad[...], NT, preferred_element_type=jnp.float32)
    for j in range(nh):
        part[j] = partial_t[j * cols:(j + 1) * cols].astype(jnp.bfloat16)
    part_c = [
        send(part.at[at_h(k)], part_in.at[h], part_s, part_r, k, {"hidden": at_h(k)}) for k in range(1, nh)
    ]

    loads[2].wait()
    pick = (
        lax.broadcasted_iota(jnp.int32, (cols, width), 1)
        == lax.broadcasted_iota(jnp.int32, (cols, width), 0) + h * cols
    ).astype(jnp.float32).astype(jnp.bfloat16)
    turned = []
    for g in range(groups):
        size = min(SPAN, rows - g * SPAN)
        piece = lax.dot_general(
            pick, table[g * SPAN:g * SPAN + size], NT, preferred_element_type=jnp.float32
        )
        if size < SPAN:
            piece = jnp.concatenate([piece, jnp.zeros((cols, SPAN - size), jnp.float32)], axis=1)
        turned.append(piece)
    quarter_t[...] = jnp.concatenate(turned, axis=0).astype(jnp.bfloat16)

    def look_up(j):
        rel = ids_all[j] - v * rows
        group = lax.shift_right_arithmetic(rel, SPAN.bit_length() - 1)
        low = jnp.bitwise_and(rel, SPAN - 1)
        hot = (lax.broadcasted_iota(jnp.int32, (SPAN, tokens), 0) == low).astype(jnp.float32).astype(jnp.bfloat16)
        one_hot[:, pl.ds(pl.multiple_of(j * tokens, tokens), tokens)] = hot
        picked = jnp.dot(quarter_t[...], hot, preferred_element_type=jnp.float32)
        total = jnp.zeros((cols, tokens), jnp.float32)
        for g in range(groups):
            total = total + jnp.where(group == g, picked[g * cols:(g + 1) * cols], 0.0)
        found[j] = total.astype(jnp.bfloat16)

    found_c = []
    for k in range(1, nv):
        ids_c[k - 1].wait_recv()
        j = at_v(nv - k)
        look_up(j)
        found_c.append(send(found.at[j], found_in.at[v], found_s, found_r, k, {"vocab": j}))
    look_up(v)

    for copy in part_c:
        copy.wait_recv()
    part_in[h] = part[h]
    token_grad = part_in[0].astype(jnp.float32)
    for j in range(1, nh):
        token_grad = token_grad + part_in[j].astype(jnp.float32)
    tg_own[...] = token_grad.astype(jnp.bfloat16)
    tg_c = [send(tg_own, tg_all.at[v], tg_s, tg_r, k, {"vocab": at_v(k)}) for k in range(1, nv)]
    tg_all[v] = tg_own[...]

    for copy in found_c:
        copy.wait_recv()
    found_in[v] = found[v]
    mine = found_in[0].astype(jnp.float32)
    for j in range(1, nv):
        mine = mine + found_in[j].astype(jnp.float32)
    emb[h] = mine.astype(jnp.bfloat16)
    emb_c = [send(emb.at[h], emb.at[h], emb_s, emb_r, k, {"hidden": at_h(k)}) for k in nearest]

    piece_c, all_c = [], []

    def start_piece(step, q):
        product = jnp.dot(emb[q], grad[...], preferred_element_type=jnp.float32)
        for j in range(nv):
            pg[step, j] = product[:, j * chunk:(j + 1) * chunk].astype(jnp.bfloat16)
        piece_c.append([
            send(pg.at[step, at_v(k)], pg_in.at[step, v], pg_s.at[step], pg_r.at[step], k, {"vocab": at_v(k)})
            for k in range(1, nv)
        ])

    def finish_piece(step, q):
        for copy in piece_c[step]:
            copy.wait_recv()
        pg_in[step, v] = pg[step, v]
        total = pg_in[step, 0].astype(jnp.float32)
        for j in range(1, nv):
            total = total + pg_in[step, j].astype(jnp.float32)
        pg_own[step] = total.astype(jnp.bfloat16)
        all_c.append([
            send(pg_own.at[step], pg_all.at[step, v], all_s.at[step], all_r.at[step], k, {"vocab": at_v(k)})
            for k in range(1, nv)
        ])
        pg_all[step, v] = pg_own[step]

    quarters = [h] + [at_h(nh - k) for k in nearest]
    start_piece(0, quarters[0])
    for step in range(1, nh):
        emb_c[step - 1].wait_recv()
        start_piece(step, quarters[step])
        finish_piece(step - 1, quarters[step - 1])
    finish_piece(nh - 1, quarters[nh - 1])

    for copy in tg_c:
        copy.wait_recv()
    for j in range(nv):
        rel = ids_all[j] - v * rows
        group = lax.shift_right_arithmetic(rel, SPAN.bit_length() - 1)
        value = tg_all[j].astype(jnp.float32)
        spread[:, j * tokens:(j + 1) * tokens] = jnp.concatenate(
            [jnp.where(group == g, value, 0.0) for g in range(groups)], axis=0
        ).astype(jnp.bfloat16)
    summed = lax.dot_general(spread[...], one_hot[...], NT, preferred_element_type=jnp.float32)
    for g in range(groups):
        size = min(SPAN, rows - g * SPAN)
        rows_out[:, g * SPAN:g * SPAN + size] = summed[g * cols:(g + 1) * cols, :size]

    for step, q in enumerate(quarters):
        for copy in all_c[step]:
            copy.wait_recv()
        proj_out[pl.ds(pl.multiple_of(q * cols, cols), cols), :] = jnp.concatenate(
            [pg_all[step, j].astype(jnp.float32) for j in range(nv)], axis=1
        )
    for copy in ids_c + part_c + tg_c + found_c + emb_c + sum(piece_c, []) + sum(all_c, []):
        copy.wait_send()


def solution(mesh):
    nv, nh = mesh.shape["vocab"], mesh.shape["hidden"]

    def on_device(token_ids, table, projection, grad_out):
        rows, width = table.shape
        tokens, hid = grad_out.shape
        cols, chunk = width // nh, hid // nv
        stacked = pl.cdiv(rows, SPAN) * cols
        half = jnp.bfloat16
        vmem = pl.BlockSpec(memory_space=pltpu.VMEM)
        hbm = pl.BlockSpec(memory_space=pl.ANY)
        sems = [pltpu.SemaphoreType.DMA((3,))]
        for peers in ((nv - 1,), (nh - 1,), (nv - 1,), (nv - 1,), (nh - 1,), (nh, nv - 1), (nh, nv - 1)):
            sems += [pltpu.SemaphoreType.DMA(peers)] * 2
        rows_t, proj_grad = pl.pallas_call(
            functools.partial(kernel, nv, nh),
            out_shape=(
                jax.ShapeDtypeStruct((cols, rows), jnp.float32),
                jax.ShapeDtypeStruct((width, hid), jnp.float32),
            ),
            in_specs=[vmem, hbm, hbm, hbm],
            out_specs=(vmem, vmem),
            scratch_shapes=[
                pltpu.VMEM((rows, width), half),
                pltpu.VMEM((width, hid), half),
                pltpu.VMEM((tokens, hid), half),
                pltpu.VMEM((nv, 1, tokens), jnp.int32),
                pltpu.VMEM((nh, cols, tokens), half),
                pltpu.VMEM((nh, cols, tokens), half),
                pltpu.VMEM((cols, tokens), half),
                pltpu.VMEM((nv, cols, tokens), half),
                pltpu.VMEM((stacked, SPAN), half),
                pltpu.VMEM((SPAN, nv * tokens), half),
                pltpu.VMEM((stacked, nv * tokens), half),
                pltpu.VMEM((nv, cols, tokens), half),
                pltpu.VMEM((nv, cols, tokens), half),
                pltpu.VMEM((nh, cols, tokens), half),
                pltpu.VMEM((nh, nv, cols, chunk), half),
                pltpu.VMEM((nh, nv, cols, chunk), half),
                pltpu.VMEM((nh, cols, chunk), half),
                pltpu.VMEM((nh, nv, cols, chunk), half),
            ] + sems,
            compiler_params=pltpu.CompilerParams(collective_id=0, has_side_effects=True),
        )(token_ids.reshape(1, tokens), table, projection, grad_out)
        return rows_t.T, proj_grad

    placed = (P("vocab"), P("vocab", None), P(None, "hidden"), P("vocab", "hidden"))
    return jax.shard_map(
        on_device,
        mesh=mesh,
        in_specs=placed,
        out_specs=(P("vocab", "hidden"), P(None, "hidden")),
        check_vma=False,
    )
```

```python
import functools

import jax
import jax.numpy as jnp
from jax import lax
from jax.experimental import pallas as pl
from jax.experimental.pallas import tpu as pltpu
from jax.sharding import PartitionSpec as P

MESH = pl.DeviceIdType.MESH
SPAN = 256
NT = (((1,), (1,)), ((), ()))


def kernel(
    nv, nh, ids_ref, table_hbm, proj_hbm, grad_hbm, rows_out, proj_out,
    table, proj, grad, ids_all, part, part_in, tg_own, tg_all, quarter_t, one_hot, spread,
    found, found_in, emb, pg, pg_in, pg_own, pg_all,
    load_sem, ids_s, ids_r, part_s, part_r, tg_s, tg_r, found_s, found_r, emb_s, emb_r, pg_s, pg_r, all_s, all_r,
):
    v = lax.axis_index("vocab")
    h = lax.axis_index("hidden")
    rows, width = table.shape
    tokens = grad.shape[0]
    cols = width // nh
    groups = pl.cdiv(rows, SPAN)
    chunk = width // nv

    loads = [
        pltpu.make_async_copy(src, dst, load_sem.at[i])
        for i, (src, dst) in enumerate(((proj_hbm, proj), (grad_hbm, grad), (table_hbm, table)))
    ]
    for load in loads:
        load.start()

    def at_v(k):
        return lax.rem(v + k, nv)

    def at_h(k):
        return lax.rem(h + k, nh)

    barrier = pltpu.get_barrier_semaphore()
    for k in range(1, nv):
        pl.semaphore_signal(barrier, inc=1, device_id={"vocab": at_v(k)}, device_id_type=MESH)
    for k in range(1, nh):
        pl.semaphore_signal(barrier, inc=1, device_id={"hidden": at_h(k)}, device_id_type=MESH)
    pl.semaphore_wait(barrier, nv + nh - 2)

    def send(src, dst, s, r, k, where):
        copy = pltpu.make_async_remote_copy(
            src_ref=src, dst_ref=dst, send_sem=s.at[k - 1], recv_sem=r.at[k - 1],
            device_id=where, device_id_type=MESH,
        )
        copy.start()
        return copy

    sent = []
    ids_c = [send(ids_ref, ids_all.at[v], ids_s, ids_r, k, {"vocab": at_v(k)}) for k in range(1, nv)]
    ids_all[v] = ids_ref[...]

    loads[0].wait()
    loads[1].wait()
    partial_t = lax.dot_general(proj[...], grad[...], NT, preferred_element_type=jnp.float32)
    for j in range(nh):
        part[j] = partial_t[j * cols:(j + 1) * cols].astype(jnp.bfloat16)
    part_c = [
        send(part.at[at_h(k)], part_in.at[h], part_s, part_r, k, {"hidden": at_h(k)}) for k in range(1, nh)
    ]

    loads[2].wait()
    pick = (
        lax.broadcasted_iota(jnp.int32, (cols, width), 1)
        == lax.broadcasted_iota(jnp.int32, (cols, width), 0) + h * cols
    ).astype(jnp.float32).astype(jnp.bfloat16)
    turned = []
    for g in range(groups):
        size = min(SPAN, rows - g * SPAN)
        piece = lax.dot_general(
            pick, table[g * SPAN:g * SPAN + size], NT, preferred_element_type=jnp.float32
        )
        if size < SPAN:
            piece = jnp.concatenate([piece, jnp.zeros((cols, SPAN - size), jnp.float32)], axis=1)
        turned.append(piece)
    quarter_t[...] = jnp.concatenate(turned, axis=0).astype(jnp.bfloat16)

    def look_up(j):
        rel = ids_all[j] - v * rows
        group = lax.shift_right_arithmetic(rel, SPAN.bit_length() - 1)
        low = jnp.bitwise_and(rel, SPAN - 1)
        hot = (lax.broadcasted_iota(jnp.int32, (SPAN, tokens), 0) == low).astype(jnp.float32).astype(jnp.bfloat16)
        one_hot[:, pl.ds(pl.multiple_of(j * tokens, tokens), tokens)] = hot
        picked = jnp.dot(quarter_t[...], hot, preferred_element_type=jnp.float32)
        total = jnp.zeros((cols, tokens), jnp.float32)
        for g in range(groups):
            total = total + jnp.where(group == g, picked[g * cols:(g + 1) * cols], 0.0)
        found[j] = total.astype(jnp.bfloat16)

    found_c = []
    for k in range(1, nv):
        ids_c[k - 1].wait_recv()
        j = at_v(nv - k)
        look_up(j)
        found_c.append(send(found.at[j], found_in.at[v], found_s, found_r, k, {"vocab": j}))
    look_up(v)

    for copy in part_c:
        copy.wait_recv()
    part_in[h] = part[h]
    token_grad = part_in[0].astype(jnp.float32)
    for j in range(1, nh):
        token_grad = token_grad + part_in[j].astype(jnp.float32)
    tg_own[...] = token_grad.astype(jnp.bfloat16)
    tg_c = [send(tg_own, tg_all.at[v], tg_s, tg_r, k, {"vocab": at_v(k)}) for k in range(1, nv)]
    tg_all[v] = tg_own[...]

    for copy in found_c:
        copy.wait_recv()
    found_in[v] = found[v]
    mine = found_in[0].astype(jnp.float32)
    for j in range(1, nv):
        mine = mine + found_in[j].astype(jnp.float32)
    emb[h] = mine.astype(jnp.bfloat16)
    emb_c = [send(emb.at[h], emb.at[h], emb_s, emb_r, k, {"hidden": at_h(k)}) for k in range(1, nh)]
    for copy in emb_c:
        copy.wait_recv()
    embedded = jnp.concatenate([emb[j].astype(jnp.float32) for j in range(nh)], axis=0).astype(jnp.bfloat16)
    partial_proj = jnp.dot(embedded, grad[...], preferred_element_type=jnp.float32)
    for j in range(nv):
        pg[j] = partial_proj[j * chunk:(j + 1) * chunk].astype(jnp.bfloat16)
    pg_c = [send(pg.at[at_v(k)], pg_in.at[v], pg_s, pg_r, k, {"vocab": at_v(k)}) for k in range(1, nv)]

    for copy in tg_c:
        copy.wait_recv()
    for j in range(nv):
        rel = ids_all[j] - v * rows
        group = lax.shift_right_arithmetic(rel, SPAN.bit_length() - 1)
        value = tg_all[j].astype(jnp.float32)
        spread[:, j * tokens:(j + 1) * tokens] = jnp.concatenate(
            [jnp.where(group == g, value, 0.0) for g in range(groups)], axis=0
        ).astype(jnp.bfloat16)
    summed = lax.dot_general(spread[...], one_hot[...], NT, preferred_element_type=jnp.float32)
    for g in range(groups):
        size = min(SPAN, rows - g * SPAN)
        rows_out[:, g * SPAN:g * SPAN + size] = summed[g * cols:(g + 1) * cols, :size]

    for copy in pg_c:
        copy.wait_recv()
    pg_in[v] = pg[v]
    total = pg_in[0].astype(jnp.float32)
    for j in range(1, nv):
        total = total + pg_in[j].astype(jnp.float32)
    pg_own[...] = total.astype(jnp.bfloat16)
    all_c = [send(pg_own, pg_all.at[v], all_s, all_r, k, {"vocab": at_v(k)}) for k in range(1, nv)]
    pg_all[v] = pg_own[...]
    for copy in all_c:
        copy.wait_recv()
    for j in range(nv):
        proj_out[j * chunk:(j + 1) * chunk] = pg_all[j].astype(jnp.float32)
    for copy in ids_c + part_c + tg_c + found_c + emb_c + pg_c + all_c:
        copy.wait_send()


def store_both(rows_in, proj_in, rows_out, proj_out, sem):
    copies = [
        pltpu.make_async_copy(src, dst, sem.at[i])
        for i, (src, dst) in enumerate(((rows_in, rows_out), (proj_in, proj_out)))
    ]
    for copy in copies:
        copy.start()
    for copy in copies:
        copy.wait()


def solution(mesh):
    nv, nh = mesh.shape["vocab"], mesh.shape["hidden"]

    def on_device(token_ids, table, projection, grad_out):
        rows, width = table.shape
        tokens, hid = grad_out.shape
        cols, chunk = width // nh, width // nv
        stacked = pl.cdiv(rows, SPAN) * cols
        half = jnp.bfloat16
        vmem = pl.BlockSpec(memory_space=pltpu.VMEM)
        hbm = pl.BlockSpec(memory_space=pl.ANY)
        sems = [pltpu.SemaphoreType.DMA((3,))]
        for peers in (nv, nh, nv, nv, nh, nv, nv):
            sems += [pltpu.SemaphoreType.DMA((peers - 1,))] * 2
        rows_t, proj_grad = pl.pallas_call(
            functools.partial(kernel, nv, nh),
            out_shape=(
                pltpu.VMEM((cols, rows), jnp.float32),
                pltpu.VMEM((width, hid), jnp.float32),
            ),
            in_specs=[vmem, hbm, hbm, hbm],
            out_specs=(vmem, vmem),
            scratch_shapes=[
                pltpu.VMEM((rows, width), half),
                pltpu.VMEM((width, hid), half),
                pltpu.VMEM((tokens, hid), half),
                pltpu.VMEM((nv, 1, tokens), jnp.int32),
                pltpu.VMEM((nh, cols, tokens), half),
                pltpu.VMEM((nh, cols, tokens), half),
                pltpu.VMEM((cols, tokens), half),
                pltpu.VMEM((nv, cols, tokens), half),
                pltpu.VMEM((stacked, SPAN), half),
                pltpu.VMEM((SPAN, nv * tokens), half),
                pltpu.VMEM((stacked, nv * tokens), half),
                pltpu.VMEM((nv, cols, tokens), half),
                pltpu.VMEM((nv, cols, tokens), half),
                pltpu.VMEM((nh, cols, tokens), half),
                pltpu.VMEM((nv, chunk, hid), half),
                pltpu.VMEM((nv, chunk, hid), half),
                pltpu.VMEM((chunk, hid), half),
                pltpu.VMEM((nv, chunk, hid), half),
            ] + sems,
            compiler_params=pltpu.CompilerParams(collective_id=0, has_side_effects=True),
        )(token_ids.reshape(1, tokens), table, projection, grad_out)
        rows_t, proj_grad = pl.pallas_call(
            store_both,
            out_shape=(
                jax.ShapeDtypeStruct((cols, rows), jnp.float32),
                jax.ShapeDtypeStruct((width, hid), jnp.float32),
            ),
            in_specs=[vmem, vmem],
            out_specs=(hbm, hbm),
            scratch_shapes=[pltpu.SemaphoreType.DMA((2,))],
        )(*(pltpu.with_memory_space_constraint(x, pltpu.VMEM) for x in (rows_t, proj_grad)))
        return rows_t.T, proj_grad

    placed = (P("vocab"), P("vocab", None), P(None, "hidden"), P("vocab", "hidden"))
    return jax.shard_map(
        on_device,
        mesh=mesh,
        in_specs=placed,
        out_specs=(P("vocab", "hidden"), P(None, "hidden")),
        check_vma=False,
    )
```

```python
import functools

import jax
import jax.numpy as jnp
from jax import lax
from jax.experimental import pallas as pl
from jax.experimental.pallas import tpu as pltpu
from jax.sharding import PartitionSpec as P

MESH = pl.DeviceIdType.MESH
SPAN = 256
NT = (((1,), (1,)), ((), ()))


def partner(index, k):
    bit = 1
    while bit <= k:
        if k & bit:
            index = index + bit - 2 * bit * lax.rem(index // bit, 2)
        bit *= 2
    return index


def far_first(n):
    return sorted(range(1, n), key=lambda k: (-bin(k // 2).count("1"), k % 2, -k))


def kernel(
    nv, nh, ids_ref, table_hbm, proj_hbm, grad_hbm, rows_out, proj_out,
    table, proj, grad, ids_all, part, part_in, tg_own, tg_all, quarter_t, one_hot, spread,
    found, found_in, emb, pg, pg_in, pg_own, pg_all,
    load_sem, ids_s, ids_r, part_s, part_r, tg_s, tg_r, found_s, found_r, emb_s, emb_r, pg_s, pg_r, all_s, all_r,
):
    v = lax.axis_index("vocab")
    h = lax.axis_index("hidden")
    rows, width = table.shape
    tokens = grad.shape[0]
    cols = width // nh
    groups = pl.cdiv(rows, SPAN)
    chunk = width // nv
    v_steps = far_first(nv)
    h_steps = sorted(range(1, nh), reverse=True)

    loads = [
        pltpu.make_async_copy(src, dst, load_sem.at[i])
        for i, (src, dst) in enumerate(((proj_hbm, proj), (grad_hbm, grad), (table_hbm, table)))
    ]
    for load in loads:
        load.start()

    def at_v(k):
        return partner(v, k)

    def at_h(k):
        return partner(h, k)

    barrier = pltpu.get_barrier_semaphore()
    for k in range(1, nv):
        pl.semaphore_signal(barrier, inc=1, device_id={"vocab": at_v(k)}, device_id_type=MESH)
    for k in range(1, nh):
        pl.semaphore_signal(barrier, inc=1, device_id={"hidden": at_h(k)}, device_id_type=MESH)
    pl.semaphore_wait(barrier, nv + nh - 2)

    def send(src, dst, s, r, k, where):
        copy = pltpu.make_async_remote_copy(
            src_ref=src, dst_ref=dst, send_sem=s.at[k - 1], recv_sem=r.at[k - 1],
            device_id=where, device_id_type=MESH,
        )
        copy.start()
        return copy

    sent = []
    ids_c = [send(ids_ref, ids_all.at[v], ids_s, ids_r, k, {"vocab": at_v(k)}) for k in v_steps]
    ids_all[v] = ids_ref[...]

    loads[0].wait()
    loads[1].wait()
    partial_t = lax.dot_general(proj[...], grad[...], NT, preferred_element_type=jnp.float32)
    for j in range(nh):
        part[j] = partial_t[j * cols:(j + 1) * cols].astype(jnp.bfloat16)
    part_c = [
        send(part.at[at_h(k)], part_in.at[h], part_s, part_r, k, {"hidden": at_h(k)}) for k in h_steps
    ]

    loads[2].wait()
    pick = (
        lax.broadcasted_iota(jnp.int32, (cols, width), 1)
        == lax.broadcasted_iota(jnp.int32, (cols, width), 0) + h * cols
    ).astype(jnp.float32).astype(jnp.bfloat16)
    turned = []
    for g in range(groups):
        size = min(SPAN, rows - g * SPAN)
        piece = lax.dot_general(
            pick, table[g * SPAN:g * SPAN + size], NT, preferred_element_type=jnp.float32
        )
        if size < SPAN:
            piece = jnp.concatenate([piece, jnp.zeros((cols, SPAN - size), jnp.float32)], axis=1)
        turned.append(piece)
    quarter_t[...] = jnp.concatenate(turned, axis=0).astype(jnp.bfloat16)

    def look_up(j):
        rel = ids_all[j] - v * rows
        group = lax.shift_right_arithmetic(rel, SPAN.bit_length() - 1)
        low = jnp.bitwise_and(rel, SPAN - 1)
        hot = (lax.broadcasted_iota(jnp.int32, (SPAN, tokens), 0) == low).astype(jnp.float32).astype(jnp.bfloat16)
        one_hot[:, pl.ds(pl.multiple_of(j * tokens, tokens), tokens)] = hot
        picked = jnp.dot(quarter_t[...], hot, preferred_element_type=jnp.float32)
        total = jnp.zeros((cols, tokens), jnp.float32)
        for g in range(groups):
            total = total + jnp.where(group == g, picked[g * cols:(g + 1) * cols], 0.0)
        found[j] = total.astype(jnp.bfloat16)

    found_c = []
    for step, k in enumerate(v_steps):
        ids_c[step].wait_recv()
        j = at_v(k)
        look_up(j)
        found_c.append(send(found.at[j], found_in.at[v], found_s, found_r, k, {"vocab": j}))
    look_up(v)

    for copy in part_c:
        copy.wait_recv()
    part_in[h] = part[h]
    token_grad = part_in[0].astype(jnp.float32)
    for j in range(1, nh):
        token_grad = token_grad + part_in[j].astype(jnp.float32)
    tg_own[...] = token_grad.astype(jnp.bfloat16)
    tg_c = [send(tg_own, tg_all.at[v], tg_s, tg_r, k, {"vocab": at_v(k)}) for k in v_steps]
    tg_all[v] = tg_own[...]

    for copy in found_c:
        copy.wait_recv()
    found_in[v] = found[v]
    mine = found_in[0].astype(jnp.float32)
    for j in range(1, nv):
        mine = mine + found_in[j].astype(jnp.float32)
    emb[h] = mine.astype(jnp.bfloat16)
    emb_c = [send(emb.at[h], emb.at[h], emb_s, emb_r, k, {"hidden": at_h(k)}) for k in h_steps]
    for copy in emb_c:
        copy.wait_recv()
    embedded = jnp.concatenate([emb[j].astype(jnp.float32) for j in range(nh)], axis=0).astype(jnp.bfloat16)
    partial_proj = jnp.dot(embedded, grad[...], preferred_element_type=jnp.float32)
    half = grad.shape[1] // 2
    pg_c = []
    for p in range(2):
        for j in range(nv):
            pg[p, j] = partial_proj[j * chunk:(j + 1) * chunk, p * half:(p + 1) * half].astype(jnp.bfloat16)
        pg_c.append([
            send(pg.at[p, at_v(k)], pg_in.at[p, v], pg_s.at[p], pg_r.at[p], k, {"vocab": at_v(k)}) for k in v_steps
        ])

    all_c = []
    for p in range(2):
        for copy in pg_c[p]:
            copy.wait_recv()
        pg_in[p, v] = pg[p, v]
        total = pg_in[p, 0].astype(jnp.float32)
        for j in range(1, nv):
            total = total + pg_in[p, j].astype(jnp.float32)
        pg_own[p] = total.astype(jnp.bfloat16)
        all_c.append([
            send(pg_own.at[p], pg_all.at[p, v], all_s.at[p], all_r.at[p], k, {"vocab": at_v(k)}) for k in v_steps
        ])
        pg_all[p, v] = pg_own[p]
    for copy in tg_c:
        copy.wait_recv()
    for j in range(nv):
        rel = ids_all[j] - v * rows
        group = lax.shift_right_arithmetic(rel, SPAN.bit_length() - 1)
        value = tg_all[j].astype(jnp.float32)
        spread[:, j * tokens:(j + 1) * tokens] = jnp.concatenate(
            [jnp.where(group == g, value, 0.0) for g in range(groups)], axis=0
        ).astype(jnp.bfloat16)
    summed = lax.dot_general(spread[...], one_hot[...], NT, preferred_element_type=jnp.float32)
    for g in range(groups):
        size = min(SPAN, rows - g * SPAN)
        rows_out[:, g * SPAN:g * SPAN + size] = summed[g * cols:(g + 1) * cols, :size]

    for p in range(2):
        for copy in all_c[p]:
            copy.wait_recv()
        for j in range(nv):
            proj_out[j * chunk:(j + 1) * chunk, p * half:(p + 1) * half] = pg_all[p, j].astype(jnp.float32)
    for copy in ids_c + part_c + tg_c + found_c + emb_c + sum(pg_c, []) + sum(all_c, []):
        copy.wait_send()


def store_both(rows_in, proj_in, rows_out, proj_out, sem):
    copies = [
        pltpu.make_async_copy(src, dst, sem.at[i])
        for i, (src, dst) in enumerate(((rows_in, rows_out), (proj_in, proj_out)))
    ]
    for copy in copies:
        copy.start()
    for copy in copies:
        copy.wait()


def solution(mesh):
    nv, nh = mesh.shape["vocab"], mesh.shape["hidden"]

    def on_device(token_ids, table, projection, grad_out):
        rows, width = table.shape
        tokens, hid = grad_out.shape
        cols, chunk = width // nh, width // nv
        stacked = pl.cdiv(rows, SPAN) * cols
        half = jnp.bfloat16
        vmem = pl.BlockSpec(memory_space=pltpu.VMEM)
        hbm = pl.BlockSpec(memory_space=pl.ANY)
        sems = [pltpu.SemaphoreType.DMA((3,))]
        for peers in ((nv - 1,), (nh - 1,), (nv - 1,), (nv - 1,), (nh - 1,), (2, nv - 1), (2, nv - 1)):
            sems += [pltpu.SemaphoreType.DMA(peers)] * 2
        rows_t, proj_grad = pl.pallas_call(
            functools.partial(kernel, nv, nh),
            out_shape=(
                pltpu.VMEM((cols, rows), jnp.float32),
                pltpu.VMEM((width, hid), jnp.float32),
            ),
            in_specs=[vmem, hbm, hbm, hbm],
            out_specs=(vmem, vmem),
            scratch_shapes=[
                pltpu.VMEM((rows, width), half),
                pltpu.VMEM((width, hid), half),
                pltpu.VMEM((tokens, hid), half),
                pltpu.VMEM((nv, 1, tokens), jnp.int32),
                pltpu.VMEM((nh, cols, tokens), half),
                pltpu.VMEM((nh, cols, tokens), half),
                pltpu.VMEM((cols, tokens), half),
                pltpu.VMEM((nv, cols, tokens), half),
                pltpu.VMEM((stacked, SPAN), half),
                pltpu.VMEM((SPAN, nv * tokens), half),
                pltpu.VMEM((stacked, nv * tokens), half),
                pltpu.VMEM((nv, cols, tokens), half),
                pltpu.VMEM((nv, cols, tokens), half),
                pltpu.VMEM((nh, cols, tokens), half),
                pltpu.VMEM((2, nv, chunk, hid // 2), half),
                pltpu.VMEM((2, nv, chunk, hid // 2), half),
                pltpu.VMEM((2, chunk, hid // 2), half),
                pltpu.VMEM((2, nv, chunk, hid // 2), half),
            ] + sems,
            compiler_params=pltpu.CompilerParams(collective_id=0, has_side_effects=True),
        )(token_ids.reshape(1, tokens), table, projection, grad_out)
        rows_t, proj_grad = pl.pallas_call(
            store_both,
            out_shape=(
                jax.ShapeDtypeStruct((cols, rows), jnp.float32),
                jax.ShapeDtypeStruct((width, hid), jnp.float32),
            ),
            in_specs=[vmem, vmem],
            out_specs=(hbm, hbm),
            scratch_shapes=[pltpu.SemaphoreType.DMA((2,))],
        )(*(pltpu.with_memory_space_constraint(x, pltpu.VMEM) for x in (rows_t, proj_grad)))
        return rows_t.T, proj_grad

    placed = (P("vocab"), P("vocab", None), P(None, "hidden"), P("vocab", "hidden"))
    return jax.shard_map(
        on_device,
        mesh=mesh,
        in_specs=placed,
        out_specs=(P("vocab", "hidden"), P(None, "hidden")),
        check_vma=False,
    )
```

```python
import functools

import jax
import jax.numpy as jnp
from jax import lax
from jax.experimental import pallas as pl
from jax.experimental.pallas import tpu as pltpu
from jax.sharding import PartitionSpec as P

MESH = pl.DeviceIdType.MESH
SPAN = 256
NT = (((1,), (1,)), ((), ()))


def partner(index, k):
    bit = 1
    while bit <= k:
        if k & bit:
            index = index + bit - 2 * bit * lax.rem(index // bit, 2)
        bit *= 2
    return index


def far_first(n):
    return sorted(range(1, n), key=lambda k: (-bin(k // 2).count("1"), k % 2, -k))


def kernel(
    nv, nh, ids_hbm, table_hbm, proj_hbm, grad_hbm, rows_out, proj_out,
    table, proj, grad, ids_all, part, part_in, tg_own, tg_all, quarter_t, one_hot, spread,
    found, found_in, emb, pg, pg_in, pg_own, pg_all,
    load_sem, ids_s, ids_r, part_s, part_r, tg_s, tg_r, found_s, found_r, emb_s, emb_r, pg_s, pg_r, all_s, all_r,
):
    v = lax.axis_index("vocab")
    h = lax.axis_index("hidden")
    rows, width = table.shape
    tokens = grad.shape[0]
    cols = width // nh
    groups = pl.cdiv(rows, SPAN)
    chunk = width // nv
    v_steps = far_first(nv)
    h_steps = sorted(range(1, nh), reverse=True)

    ids_load = pltpu.make_async_copy(ids_hbm, ids_all.at[v], load_sem.at[3])
    ids_load.start()
    loads = [
        pltpu.make_async_copy(src, dst, load_sem.at[i])
        for i, (src, dst) in enumerate(((proj_hbm, proj), (grad_hbm, grad), (table_hbm, table)))
    ]
    def at_v(k):
        return partner(v, k)

    def at_h(k):
        return partner(h, k)

    barrier = pltpu.get_barrier_semaphore()
    for k in range(1, nv):
        pl.semaphore_signal(barrier, inc=1, device_id={"vocab": at_v(k)}, device_id_type=MESH)
    for k in range(1, nh):
        pl.semaphore_signal(barrier, inc=1, device_id={"hidden": at_h(k)}, device_id_type=MESH)
    for load in loads:
        load.start()
    pl.semaphore_wait(barrier, nv + nh - 2)

    def send(src, dst, s, r, k, where):
        copy = pltpu.make_async_remote_copy(
            src_ref=src, dst_ref=dst, send_sem=s.at[k - 1], recv_sem=r.at[k - 1],
            device_id=where, device_id_type=MESH,
        )
        copy.start()
        return copy

    ids_load.wait()
    ids_c = [send(ids_all.at[v], ids_all.at[v], ids_s, ids_r, k, {"vocab": at_v(k)}) for k in v_steps]

    loads[0].wait()
    loads[1].wait()
    partial_t = lax.dot_general(proj[...], grad[...], NT, preferred_element_type=jnp.float32)
    for j in range(nh):
        part[j] = partial_t[j * cols:(j + 1) * cols].astype(jnp.bfloat16)
    part_c = [
        send(part.at[at_h(k)], part_in.at[h], part_s, part_r, k, {"hidden": at_h(k)}) for k in h_steps
    ]

    loads[2].wait()
    pick = (
        lax.broadcasted_iota(jnp.int32, (cols, width), 1)
        == lax.broadcasted_iota(jnp.int32, (cols, width), 0) + h * cols
    ).astype(jnp.float32).astype(jnp.bfloat16)
    turned = []
    for g in range(groups):
        size = min(SPAN, rows - g * SPAN)
        piece = lax.dot_general(
            pick, table[g * SPAN:g * SPAN + size], NT, preferred_element_type=jnp.float32
        )
        if size < SPAN:
            piece = jnp.concatenate([piece, jnp.zeros((cols, SPAN - size), jnp.float32)], axis=1)
        turned.append(piece)
    quarter_t[...] = jnp.concatenate(turned, axis=0).astype(jnp.bfloat16)

    def look_up(j):
        rel = ids_all[j] - v * rows
        group = lax.shift_right_arithmetic(rel, SPAN.bit_length() - 1)
        low = jnp.bitwise_and(rel, SPAN - 1)
        hot = (lax.broadcasted_iota(jnp.int32, (SPAN, tokens), 0) == low).astype(jnp.float32).astype(jnp.bfloat16)
        one_hot[:, pl.ds(pl.multiple_of(j * tokens, tokens), tokens)] = hot
        picked = jnp.dot(quarter_t[...], hot, preferred_element_type=jnp.float32)
        total = jnp.zeros((cols, tokens), jnp.float32)
        for g in range(groups):
            total = total + jnp.where(group == g, picked[g * cols:(g + 1) * cols], 0.0)
        found[j] = total.astype(jnp.bfloat16)

    found_c = []
    for step, k in enumerate(v_steps):
        ids_c[step].wait_recv()
        j = at_v(k)
        look_up(j)
        found_c.append(send(found.at[j], found_in.at[v], found_s, found_r, k, {"vocab": j}))
    look_up(v)

    for copy in part_c:
        copy.wait_recv()
    part_in[h] = part[h]
    token_grad = part_in[0].astype(jnp.float32)
    for j in range(1, nh):
        token_grad = token_grad + part_in[j].astype(jnp.float32)
    tg_own[...] = token_grad.astype(jnp.bfloat16)
    tg_c = [send(tg_own, tg_all.at[v], tg_s, tg_r, k, {"vocab": at_v(k)}) for k in v_steps]
    tg_all[v] = tg_own[...]

    for copy in found_c:
        copy.wait_recv()
    found_in[v] = found[v]
    mine = found_in[0].astype(jnp.float32)
    for j in range(1, nv):
        mine = mine + found_in[j].astype(jnp.float32)
    emb[h] = mine.astype(jnp.bfloat16)
    emb_c = [send(emb.at[h], emb.at[h], emb_s, emb_r, k, {"hidden": at_h(k)}) for k in h_steps]
    for copy in emb_c:
        copy.wait_recv()
    embedded = jnp.concatenate([emb[j].astype(jnp.float32) for j in range(nh)], axis=0).astype(jnp.bfloat16)
    partial_proj = jnp.dot(embedded, grad[...], preferred_element_type=jnp.float32)
    half = grad.shape[1] // 2
    pg_c = []
    for p in range(2):
        for j in range(nv):
            pg[p, j] = partial_proj[j * chunk:(j + 1) * chunk, p * half:(p + 1) * half].astype(jnp.bfloat16)
        pg_c.append([
            send(pg.at[p, at_v(k)], pg_in.at[p, v], pg_s.at[p], pg_r.at[p], k, {"vocab": at_v(k)}) for k in v_steps
        ])

    all_c = []
    for p in range(2):
        for copy in pg_c[p]:
            copy.wait_recv()
        pg_in[p, v] = pg[p, v]
        total = pg_in[p, 0].astype(jnp.float32)
        for j in range(1, nv):
            total = total + pg_in[p, j].astype(jnp.float32)
        pg_own[p] = total.astype(jnp.bfloat16)
        all_c.append([
            send(pg_own.at[p], pg_all.at[p, v], all_s.at[p], all_r.at[p], k, {"vocab": at_v(k)}) for k in v_steps
        ])
        pg_all[p, v] = pg_own[p]
    for copy in tg_c:
        copy.wait_recv()
    for j in range(nv):
        rel = ids_all[j] - v * rows
        group = lax.shift_right_arithmetic(rel, SPAN.bit_length() - 1)
        value = tg_all[j].astype(jnp.float32)
        spread[:, j * tokens:(j + 1) * tokens] = jnp.concatenate(
            [jnp.where(group == g, value, 0.0) for g in range(groups)], axis=0
        ).astype(jnp.bfloat16)
    summed = lax.dot_general(spread[...], one_hot[...], NT, preferred_element_type=jnp.float32)
    for g in range(groups):
        size = min(SPAN, rows - g * SPAN)
        rows_out[:, g * SPAN:g * SPAN + size] = summed[g * cols:(g + 1) * cols, :size]

    for p in range(2):
        for copy in all_c[p]:
            copy.wait_recv()
        for j in range(nv):
            proj_out[j * chunk:(j + 1) * chunk, p * half:(p + 1) * half] = pg_all[p, j].astype(jnp.float32)
    for copy in ids_c + part_c + tg_c + found_c + emb_c + sum(pg_c, []) + sum(all_c, []):
        copy.wait_send()


def store_both(rows_in, proj_in, rows_out, proj_out, sem):
    copies = [
        pltpu.make_async_copy(src, dst, sem.at[i])
        for i, (src, dst) in enumerate(((rows_in, rows_out), (proj_in, proj_out)))
    ]
    for copy in copies:
        copy.start()
    for copy in copies:
        copy.wait()


def solution(mesh):
    nv, nh = mesh.shape["vocab"], mesh.shape["hidden"]

    def on_device(token_ids, table, projection, grad_out):
        rows, width = table.shape
        tokens, hid = grad_out.shape
        cols, chunk = width // nh, width // nv
        stacked = pl.cdiv(rows, SPAN) * cols
        half = jnp.bfloat16
        vmem = pl.BlockSpec(memory_space=pltpu.VMEM)
        hbm = pl.BlockSpec(memory_space=pl.ANY)
        sems = [pltpu.SemaphoreType.DMA((4,))]
        for peers in ((nv - 1,), (nh - 1,), (nv - 1,), (nv - 1,), (nh - 1,), (2, nv - 1), (2, nv - 1)):
            sems += [pltpu.SemaphoreType.DMA(peers)] * 2
        rows_t, proj_grad = pl.pallas_call(
            functools.partial(kernel, nv, nh),
            out_shape=(
                pltpu.VMEM((cols, rows), jnp.float32),
                pltpu.VMEM((width, hid), jnp.float32),
            ),
            in_specs=[hbm, hbm, hbm, hbm],
            out_specs=(vmem, vmem),
            scratch_shapes=[
                pltpu.VMEM((rows, width), half),
                pltpu.VMEM((width, hid), half),
                pltpu.VMEM((tokens, hid), half),
                pltpu.VMEM((nv, 1, tokens), jnp.int32),
                pltpu.VMEM((nh, cols, tokens), half),
                pltpu.VMEM((nh, cols, tokens), half),
                pltpu.VMEM((cols, tokens), half),
                pltpu.VMEM((nv, cols, tokens), half),
                pltpu.VMEM((stacked, SPAN), half),
                pltpu.VMEM((SPAN, nv * tokens), half),
                pltpu.VMEM((stacked, nv * tokens), half),
                pltpu.VMEM((nv, cols, tokens), half),
                pltpu.VMEM((nv, cols, tokens), half),
                pltpu.VMEM((nh, cols, tokens), half),
                pltpu.VMEM((2, nv, chunk, hid // 2), half),
                pltpu.VMEM((2, nv, chunk, hid // 2), half),
                pltpu.VMEM((2, chunk, hid // 2), half),
                pltpu.VMEM((2, nv, chunk, hid // 2), half),
            ] + sems,
            compiler_params=pltpu.CompilerParams(collective_id=0, has_side_effects=True),
        )(token_ids.reshape(1, tokens), table, projection, grad_out)
        rows_t, proj_grad = pl.pallas_call(
            store_both,
            out_shape=(
                jax.ShapeDtypeStruct((cols, rows), jnp.float32),
                jax.ShapeDtypeStruct((width, hid), jnp.float32),
            ),
            in_specs=[vmem, vmem],
            out_specs=(hbm, hbm),
            scratch_shapes=[pltpu.SemaphoreType.DMA((2,))],
        )(*(pltpu.with_memory_space_constraint(x, pltpu.VMEM) for x in (rows_t, proj_grad)))
        return rows_t.T, proj_grad

    placed = (P("vocab"), P("vocab", None), P(None, "hidden"), P("vocab", "hidden"))
    return jax.shard_map(
        on_device,
        mesh=mesh,
        in_specs=placed,
        out_specs=(P("vocab", "hidden"), P(None, "hidden")),
        check_vma=False,
    )
```

```python
import functools

import jax
import jax.numpy as jnp
from jax import lax
from jax.experimental import pallas as pl
from jax.experimental.pallas import tpu as pltpu
from jax.sharding import PartitionSpec as P

MESH = pl.DeviceIdType.MESH
SPAN = 256
NT = (((1,), (1,)), ((), ()))


def partner(index, k):
    bit = 1
    while bit <= k:
        if k & bit:
            index = index + bit - 2 * bit * lax.rem(index // bit, 2)
        bit *= 2
    return index


def far_first(n):
    return sorted(range(1, n), key=lambda k: (-bin(k // 2).count("1"), k % 2, -k))


def kernel(
    nv, nh, ids_hbm, table_hbm, proj_hbm, grad_hbm, rows_out, proj_out,
    table, proj, grad, ids_all, part, part_in, tg_own, tg_all, quarter_t, one_hot, spread,
    found, found_in, emb, pg, pg_in, pg_own, pg_all,
    load_sem, ids_s, ids_r, part_s, part_r, tg_s, tg_r, found_s, found_r, emb_s, emb_r, pg_s, pg_r, all_s, all_r,
):
    v = lax.axis_index("vocab")
    h = lax.axis_index("hidden")
    rows, width = table.shape
    tokens = grad.shape[0]
    cols = width // nh
    groups = pl.cdiv(rows, SPAN)
    chunk = width // nv
    v_steps = far_first(nv)
    h_steps = sorted(range(1, nh), reverse=True)

    ids_load = pltpu.make_async_copy(ids_hbm, ids_all.at[v], load_sem.at[3])
    ids_load.start()
    loads = [
        pltpu.make_async_copy(src, dst, load_sem.at[i])
        for i, (src, dst) in enumerate(((proj_hbm, proj), (grad_hbm, grad), (table_hbm, table)))
    ]
    def at_v(k):
        return partner(v, k)

    def at_h(k):
        return partner(h, k)

    barrier = pltpu.get_barrier_semaphore()
    for k in range(1, nv):
        pl.semaphore_signal(barrier, inc=1, device_id={"vocab": at_v(k)}, device_id_type=MESH)
    for k in range(1, nh):
        pl.semaphore_signal(barrier, inc=1, device_id={"hidden": at_h(k)}, device_id_type=MESH)
    for load in loads:
        load.start()
    pl.semaphore_wait(barrier, nv + nh - 2)

    def send(src, dst, s, r, k, where):
        copy = pltpu.make_async_remote_copy(
            src_ref=src, dst_ref=dst, send_sem=s.at[k - 1], recv_sem=r.at[k - 1],
            device_id=where, device_id_type=MESH,
        )
        copy.start()
        return copy

    ids_load.wait()
    ids_c = [send(ids_all.at[v], ids_all.at[v], ids_s, ids_r, k, {"vocab": at_v(k)}) for k in v_steps]

    loads[0].wait()
    loads[1].wait()
    partial_t = lax.dot_general(proj[...], grad[...], NT, preferred_element_type=jnp.float32)
    for j in range(nh):
        part[j] = partial_t[j * cols:(j + 1) * cols].astype(jnp.bfloat16)
    part_c = [
        send(part.at[at_h(k)], part_in.at[h], part_s, part_r, k, {"hidden": at_h(k)}) for k in h_steps
    ]

    loads[2].wait()
    pick = (
        lax.broadcasted_iota(jnp.int32, (cols, width), 1)
        == lax.broadcasted_iota(jnp.int32, (cols, width), 0) + h * cols
    ).astype(jnp.float32).astype(jnp.bfloat16)
    turned = []
    for g in range(groups):
        size = min(SPAN, rows - g * SPAN)
        piece = lax.dot_general(
            pick, table[g * SPAN:g * SPAN + size], NT, preferred_element_type=jnp.float32
        )
        if size < SPAN:
            piece = jnp.concatenate([piece, jnp.zeros((cols, SPAN - size), jnp.float32)], axis=1)
        turned.append(piece)
    quarter_t[...] = jnp.concatenate(turned, axis=0).astype(jnp.bfloat16)

    def look_up(j):
        rel = ids_all[j] - v * rows
        group = lax.shift_right_arithmetic(rel, SPAN.bit_length() - 1)
        low = jnp.bitwise_and(rel, SPAN - 1)
        hot = (lax.broadcasted_iota(jnp.int32, (SPAN, tokens), 0) == low).astype(jnp.float32).astype(jnp.bfloat16)
        one_hot[:, pl.ds(pl.multiple_of(j * tokens, tokens), tokens)] = hot
        picked = jnp.dot(quarter_t[...], hot, preferred_element_type=jnp.float32)
        total = jnp.zeros((cols, tokens), jnp.float32)
        for g in range(groups):
            total = total + jnp.where(group == g, picked[g * cols:(g + 1) * cols], 0.0)
        found[j] = total.astype(jnp.bfloat16)

    found_c = []
    for step, k in enumerate(v_steps):
        ids_c[step].wait_recv()
        j = at_v(k)
        look_up(j)
        found_c.append(send(found.at[j], found_in.at[v], found_s, found_r, k, {"vocab": j}))
    look_up(v)

    for copy in found_c:
        copy.wait_recv()
    found_in[v] = found[v]
    mine = found_in[0].astype(jnp.float32)
    for j in range(1, nv):
        mine = mine + found_in[j].astype(jnp.float32)
    emb[h] = mine.astype(jnp.bfloat16)
    emb_c = [send(emb.at[h], emb.at[h], emb_s, emb_r, k, {"hidden": at_h(k)}) for k in h_steps]

    for copy in part_c:
        copy.wait_recv()
    part_in[h] = part[h]
    token_grad = part_in[0].astype(jnp.float32)
    for j in range(1, nh):
        token_grad = token_grad + part_in[j].astype(jnp.float32)
    tg_own[...] = token_grad.astype(jnp.bfloat16)
    tg_c = [send(tg_own, tg_all.at[v], tg_s, tg_r, k, {"vocab": at_v(k)}) for k in v_steps]
    tg_all[v] = tg_own[...]

    for copy in emb_c:
        copy.wait_recv()
    embedded = jnp.concatenate([emb[j].astype(jnp.float32) for j in range(nh)], axis=0).astype(jnp.bfloat16)
    partial_proj = jnp.dot(embedded, grad[...], preferred_element_type=jnp.float32)
    half = grad.shape[1] // 2
    pg_c = []
    for p in range(2):
        for j in range(nv):
            pg[p, j] = partial_proj[j * chunk:(j + 1) * chunk, p * half:(p + 1) * half].astype(jnp.bfloat16)
        pg_c.append([
            send(pg.at[p, at_v(k)], pg_in.at[p, v], pg_s.at[p], pg_r.at[p], k, {"vocab": at_v(k)}) for k in v_steps
        ])

    all_c = []
    for p in range(2):
        for copy in pg_c[p]:
            copy.wait_recv()
        pg_in[p, v] = pg[p, v]
        total = pg_in[p, 0].astype(jnp.float32)
        for j in range(1, nv):
            total = total + pg_in[p, j].astype(jnp.float32)
        pg_own[p] = total.astype(jnp.bfloat16)
        all_c.append([
            send(pg_own.at[p], pg_all.at[p, v], all_s.at[p], all_r.at[p], k, {"vocab": at_v(k)}) for k in v_steps
        ])
        pg_all[p, v] = pg_own[p]
    for copy in tg_c:
        copy.wait_recv()
    for j in range(nv):
        rel = ids_all[j] - v * rows
        group = lax.shift_right_arithmetic(rel, SPAN.bit_length() - 1)
        value = tg_all[j].astype(jnp.float32)
        spread[:, j * tokens:(j + 1) * tokens] = jnp.concatenate(
            [jnp.where(group == g, value, 0.0) for g in range(groups)], axis=0
        ).astype(jnp.bfloat16)
    summed = lax.dot_general(spread[...], one_hot[...], NT, preferred_element_type=jnp.float32)
    for g in range(groups):
        size = min(SPAN, rows - g * SPAN)
        rows_out[:, g * SPAN:g * SPAN + size] = summed[g * cols:(g + 1) * cols, :size]

    for p in range(2):
        for copy in all_c[p]:
            copy.wait_recv()
        for j in range(nv):
            proj_out[j * chunk:(j + 1) * chunk, p * half:(p + 1) * half] = pg_all[p, j].astype(jnp.float32)
    for copy in ids_c + part_c + tg_c + found_c + emb_c + sum(pg_c, []) + sum(all_c, []):
        copy.wait_send()


def store_both(rows_in, proj_in, rows_out, proj_out, sem):
    copies = [
        pltpu.make_async_copy(src, dst, sem.at[i])
        for i, (src, dst) in enumerate(((rows_in, rows_out), (proj_in, proj_out)))
    ]
    for copy in copies:
        copy.start()
    for copy in copies:
        copy.wait()


def solution(mesh):
    nv, nh = mesh.shape["vocab"], mesh.shape["hidden"]

    def on_device(token_ids, table, projection, grad_out):
        rows, width = table.shape
        tokens, hid = grad_out.shape
        cols, chunk = width // nh, width // nv
        stacked = pl.cdiv(rows, SPAN) * cols
        half = jnp.bfloat16
        vmem = pl.BlockSpec(memory_space=pltpu.VMEM)
        hbm = pl.BlockSpec(memory_space=pl.ANY)
        sems = [pltpu.SemaphoreType.DMA((4,))]
        for peers in ((nv - 1,), (nh - 1,), (nv - 1,), (nv - 1,), (nh - 1,), (2, nv - 1), (2, nv - 1)):
            sems += [pltpu.SemaphoreType.DMA(peers)] * 2
        rows_t, proj_grad = pl.pallas_call(
            functools.partial(kernel, nv, nh),
            out_shape=(
                pltpu.VMEM((cols, rows), jnp.float32),
                pltpu.VMEM((width, hid), jnp.float32),
            ),
            in_specs=[hbm, hbm, hbm, hbm],
            out_specs=(vmem, vmem),
            scratch_shapes=[
                pltpu.VMEM((rows, width), half),
                pltpu.VMEM((width, hid), half),
                pltpu.VMEM((tokens, hid), half),
                pltpu.VMEM((nv, 1, tokens), jnp.int32),
                pltpu.VMEM((nh, cols, tokens), half),
                pltpu.VMEM((nh, cols, tokens), half),
                pltpu.VMEM((cols, tokens), half),
                pltpu.VMEM((nv, cols, tokens), half),
                pltpu.VMEM((stacked, SPAN), half),
                pltpu.VMEM((SPAN, nv * tokens), half),
                pltpu.VMEM((stacked, nv * tokens), half),
                pltpu.VMEM((nv, cols, tokens), half),
                pltpu.VMEM((nv, cols, tokens), half),
                pltpu.VMEM((nh, cols, tokens), half),
                pltpu.VMEM((2, nv, chunk, hid // 2), half),
                pltpu.VMEM((2, nv, chunk, hid // 2), half),
                pltpu.VMEM((2, chunk, hid // 2), half),
                pltpu.VMEM((2, nv, chunk, hid // 2), half),
            ] + sems,
            compiler_params=pltpu.CompilerParams(collective_id=0, has_side_effects=True),
        )(token_ids.reshape(1, tokens), table, projection, grad_out)
        rows_t, proj_grad = pl.pallas_call(
            store_both,
            out_shape=(
                jax.ShapeDtypeStruct((cols, rows), jnp.float32),
                jax.ShapeDtypeStruct((width, hid), jnp.float32),
            ),
            in_specs=[vmem, vmem],
            out_specs=(hbm, hbm),
            scratch_shapes=[pltpu.SemaphoreType.DMA((2,))],
        )(*(pltpu.with_memory_space_constraint(x, pltpu.VMEM) for x in (rows_t, proj_grad)))
        return rows_t.T, proj_grad

    placed = (P("vocab"), P("vocab", None), P(None, "hidden"), P("vocab", "hidden"))
    return jax.shard_map(
        on_device,
        mesh=mesh,
        in_specs=placed,
        out_specs=(P("vocab", "hidden"), P(None, "hidden")),
        check_vma=False,
    )
```
